1024 devices in a mesh: row: 16 (over z_hi, y), col: 64 (over z_lo, x, core).
Axes of the slice: x: 8, y: 8, z: 8 (z_hi: 2, z_lo: 4; z = z_hi * 4 + z_lo), core: 2. Of those that a mesh axis runs over, the one named last changes fastest.
Arguments:
- query_states: bfloat16 [16, 64, 128, 768], P('row', 'col'), may hold values from -15 to 15
- key_states: bfloat16 [16, 64, 128, 768], P('row', 'col'), may hold values from -6 to 6
- value_states: bfloat16 [16, 64, 128, 768], P('row', 'col'), may hold values from -6 to 6
- tissue_map: int32 [16, 64], replicated, may hold values 0 or 1
Outputs:
- attended: bfloat16 [16, 64, 128, 768], P('row', 'col')
The draws below stay inside these ranges and needn't reach their ends.
All inputs are finite; a program needn't handle non-finite values.
Results may differ from the reference program's by a relative error of at most 0.0032.
Values may be sent and summed in bfloat16 or wider, within the bound.
No kernel may reach another device: no remote copies, remote signals or barrier semaphores. Data moves between devices by JAX's collectives and lax.ppermute only.
A program may use at most 32 MiB of HBM per device.

```python
import jax
import jax.numpy as jnp
from jax import lax

HDIM = 64
HEADS = 12
TOK_TILE = 128
TR = 16
TC = 64
HD = 768


def draw_query_states(key, part):
    sample = 2.5 * jax.random.truncated_normal(jax.random.fold_in(key, 1), -6.0, 6.0, (TR, TC, TOK_TILE, HEADS * HDIM))
    return sample.astype(jnp.bfloat16)


def draw_key_states(key, part):
    sample = jax.random.truncated_normal(jax.random.fold_in(key, 2), -6.0, 6.0, (TR, TC, TOK_TILE, HEADS * HDIM))
    return sample.astype(jnp.bfloat16)


def touch_ends(entries, stream_key, least, top_value):
    shape = entries.shape
    place = [jax.random.randint(jax.random.fold_in(stream_key, axis), (), 0, shape[axis]) for axis in range(len(shape))]
    entries = entries.at[tuple(place)].set(least)
    longest = shape.index(max(shape))
    place[longest] = (place[longest] + 1) % shape[longest]
    return entries.at[tuple(place)].set(top_value)


def shard_levels(stream_key, shape, pieces, least, high):
    loudness, own = 1.0, jax.random.fold_in(stream_key, 6)
    for axis_at, shards_of in pieces:
        steps = jnp.exp(jax.random.uniform(jax.random.fold_in(own, axis_at), (shards_of,), jnp.float32, least / len(pieces), high / len(pieces)))
        loudness = loudness * jnp.repeat(steps, shape[axis_at] // shards_of).reshape([-1 if axis == axis_at else 1 for axis in range(len(shape))])
    return loudness


def scatter_about(key, shape, scale, bound, shards=(), kind=jnp.bfloat16):
    array = scale * jax.random.normal(key, shape, jnp.float32)
    if shards:
        array = array * shard_levels(key, shape, shards, -0.22, 0.18)
    return jnp.clip(array, -bound, bound).astype(kind)


def setup_inputs(seed: int = 0) -> dict:
    arg_keys = jax.random.split(jax.random.key(seed), 5)
    return {
        "query_states": draw_query_states(jax.random.fold_in(arg_keys[4], 71), 0),
        "key_states": draw_key_states(jax.random.fold_in(arg_keys[4], 71), 0),
        "value_states": scatter_about(arg_keys[2], (TR, TC, TOK_TILE, HD), 1.0, 6.0, ((0, 16), (1, 64))),
        "tissue_map": touch_ends((jax.random.randint(arg_keys[3], (TR, TC), 0, 4) < 3).astype(jnp.int32), jax.random.fold_in(arg_keys[3], 1), 0, 1),
    }


def reference(query_states, key_states, value_states, tissue_map):
    score_scale = HDIM ** -0.5
    tile_pad = ((1, 1), (1, 1), (0, 0), (0, 0))
    keys_padded = jnp.pad(key_states, tile_pad)
    values_padded = jnp.pad(value_states, tile_pad)
    tissue_padded = jnp.pad(tissue_map, 1)
    centre = jnp.arange(9) == 4

    def one_tile(tile_index):
        row_at = (tile_index // TC).astype(jnp.int32)
        col_at = (tile_index % TC).astype(jnp.int32)
        zero = jnp.zeros((), jnp.int32)
        query_tile = lax.dynamic_slice(query_states, (row_at, col_at, zero, zero), (1, 1, TOK_TILE, HD))
        query_tile = query_tile.reshape(TOK_TILE, HEADS, HDIM).astype(jnp.float32)
        near_keys = lax.dynamic_slice(keys_padded, (row_at, col_at, zero, zero), (3, 3, TOK_TILE, HD))
        near_keys = near_keys.reshape(9 * TOK_TILE, HEADS, HDIM).astype(jnp.float32)
        near_values = lax.dynamic_slice(values_padded, (row_at, col_at, zero, zero), (3, 3, TOK_TILE, HD))
        near_values = near_values.reshape(9 * TOK_TILE, HEADS, HDIM).astype(jnp.float32)
        markers = lax.dynamic_slice(tissue_padded, (row_at, col_at), (3, 3)).reshape(9)
        present = (markers > 0) | centre
        key_keep = jnp.repeat(present, TOK_TILE)
        scores = jnp.einsum("qhd,khd->hqk", query_tile, near_keys) * score_scale
        scores = jnp.where(key_keep[None, None, :], scores, -jnp.inf)
        row_top = jnp.max(scores, axis=-1, keepdims=True)
        weights = jnp.exp(scores - row_top)
        totals = jnp.sum(weights, axis=-1)
        rounded = lax.optimization_barrier(weights.astype(jnp.bfloat16)).astype(jnp.float32)
        mixed = jnp.einsum("hqk,khd->qhd", rounded, near_values)
        mixed = mixed / jnp.transpose(totals)[:, :, None]
        own_tile = markers[4].astype(jnp.float32)
        return (mixed * own_tile).reshape(TOK_TILE, HD).astype(jnp.bfloat16)

    attended = lax.map(one_tile, jnp.arange(TR * TC, dtype=jnp.int32))
    return attended.reshape(TR, TC, TOK_TILE, HD)
```

```python
import functools

import jax
import jax.numpy as jnp
from jax import lax
from jax.experimental import pallas as pl
from jax.experimental.pallas import tpu as pltpu
from jax.sharding import PartitionSpec as P

HDIM = 64
HEADS = 12
PAIR = 2 * HDIM
PAIRS = HEADS // 2
TOK = 128
HD = HEADS * HDIM
LOG2E = 1.4426950408889634
SCALE = HDIM ** (-0.5) * LOG2E
NEG = -1e30
FLOOR = -1e20
VMEM = pl.BlockSpec(memory_space=pltpu.VMEM)
SMEM = pl.BlockSpec(memory_space=pltpu.SMEM)
F32 = jnp.float32
BF16 = jnp.bfloat16


def swaps(count, first):
    pairs = []
    for i in range(first, count - 1, 2):
        pairs += [(i, i + 1), (i + 1, i)]
    return pairs


def partner(i, odd):
    return ((i + 1) ^ 1) - 1 if odd else i ^ 1


def lane_low():
    return lax.broadcasted_iota(jnp.int32, (TOK, PAIR), 1) < HDIM


def position():
    return lax.axis_index("row"), lax.axis_index("col")


def tile_bias(tissue, row, col):
    rows, cols = tissue.shape
    inside = (row >= 0) & (row < rows)
    at = tissue[jnp.clip(row, 0, rows - 1), col]
    return jnp.where(inside & (at > 0), 0.0, NEG).astype(F32)


def attend_pair(query, keys, values, biases, low):
    zero = jnp.zeros_like(query)
    both = jnp.concatenate([jnp.where(low, query, zero), jnp.where(low, zero, query)], axis=0)
    scores = []
    for key, bias in zip(keys, biases):
        s = lax.dot_general(both, key, (((1,), (1,)), ((), ())), preferred_element_type=F32) * SCALE
        scores.append(s if bias is None else s + bias)
    top = functools.reduce(jnp.maximum, scores)
    top = jnp.maximum(jnp.max(top, axis=1, keepdims=True), FLOOR)
    weights = [jnp.exp2(s - top) for s in scores]
    total = jnp.sum(functools.reduce(jnp.add, weights), axis=1, keepdims=True)
    mixed = functools.reduce(
        jnp.add,
        [jnp.dot(w.astype(BF16), v, preferred_element_type=F32) for w, v in zip(weights, values)],
    )
    shape = (TOK, PAIR)
    top2 = jnp.where(low, jnp.broadcast_to(top[:TOK], shape), jnp.broadcast_to(top[TOK:], shape))
    tot2 = jnp.where(low, jnp.broadcast_to(total[:TOK], shape), jnp.broadcast_to(total[TOK:], shape))
    mix2 = jnp.where(low, mixed[:TOK], mixed[TOK:])
    return top2, tot2, mix2


def lanes(p):
    return slice(p * PAIR, (p + 1) * PAIR)


def early_kernel(tissue, q, qc, qd, k, v, ka, va, top_ref, tot_ref, mix_ref):
    row, col = position()
    low = lane_low()
    own = tile_bias(tissue, row, col)
    near = tile_bias(tissue, partner(row, False), col)
    for i, query in enumerate((q, qc, qd)):
        for p in range(PAIRS):
            at = lanes(p)
            t, l, m = attend_pair(
                query[:, at], (k[:, at], ka[:, at]), (v[:, at], va[:, at]),
                (None if i == 0 else own, near), low,
            )
            top_ref[i, :, at] = t
            tot_ref[i, :, at] = l
            mix_ref[i, :, at] = m


def late_part(query, kvb, bias, top, tot, mix, i, p, low):
    at = lanes(p)
    t, l, m = attend_pair(query[:, at], (kvb[0, :, at],), (kvb[1, :, at],), (bias,), low)
    t0 = top[i, :, at]
    best = jnp.maximum(t, t0)
    new, old = jnp.exp2(t - best), jnp.exp2(t0 - best)
    return best, l * new + tot[i, :, at] * old, m * new + mix[i, :, at] * old


def spot(p):
    return (lax.broadcasted_iota(jnp.int32, (TOK, PAIR), 1) & (HDIM - 1)) == p


def pieces(x, count):
    parts = []
    for _ in range(count):
        part = x.astype(BF16).astype(F32)
        parts.append(part)
        x = x - part
    return parts


def side_kernel(tissue, qc, qd, kvb, top, tot, mix, out_c, out_d):
    row, col = position()
    low = lane_low()
    bias = tile_bias(tissue, partner(row, True), col)
    for i, (query, out) in enumerate(((qc, out_c), (qd, out_d))):
        stats = jnp.zeros((TOK, PAIR), F32)
        for p in range(PAIRS):
            best, total, mixed = late_part(query, kvb, bias, top, tot, mix, i + 1, p, low)
            out[:, lanes(p)] = mixed.astype(BF16)
            for slot, piece in enumerate(pieces(best, 3) + pieces(total, 2)):
                stats = jnp.where(spot(p + 8 * slot), piece, stats)
        out[:, HD:] = stats.astype(BF16)


def own_kernel(tissue, q, kvb, top, tot, mix, mix_out, top_out, tot_out):
    row, col = position()
    low = lane_low()
    bias = tile_bias(tissue, partner(row, True), col)
    tops = jnp.zeros((TOK, PAIR), F32)
    tots = jnp.ones((TOK, PAIR), F32)
    for p in range(PAIRS):
        best, total, mixed = late_part(q, kvb, bias, top, tot, mix, 0, p, low)
        mix_out[:, lanes(p)] = mixed
        tops = jnp.where(spot(p), best, tops)
        tots = jnp.where(spot(p), total, tots)
    top_out[...] = tops
    tot_out[...] = tots


def merge_kernel(cols, tissue, mix, top, tot, in_c, in_d, out):
    row, col = position()
    low = lane_low()
    own = jnp.where(tissue[row, col] > 0, 1.0, 0.0).astype(F32)
    other = partner(col, True)
    missing = jnp.where((other >= 0) & (other < cols), 0.0, NEG).astype(F32)
    tops, tots = [top[...]], [tot[...]]
    for part, gap in ((in_c, None), (in_d, missing)):
        stats = part[:, HD:].astype(F32)
        slots = [stats] + [pltpu.roll(stats, PAIR - 8 * slot, 1) for slot in range(1, 5)]
        highest = slots[0] + slots[1] + slots[2]
        tops.append(highest if gap is None else highest + gap)
        tots.append(slots[3] + slots[4])
    best = functools.reduce(jnp.maximum, tops)
    shares = [jnp.exp2(t - best) for t in tops]
    total = functools.reduce(jnp.add, [s * t for s, t in zip(shares, tots)])
    shares = [s * own / total for s in shares]
    for p in range(PAIRS):
        at = lanes(p)
        acc = None
        for share, part in zip(shares, (mix, in_c, in_d)):
            shape = (TOK, PAIR)
            factor = jnp.where(
                low,
                jnp.broadcast_to(share[:, p : p + 1], shape),
                jnp.broadcast_to(share[:, HDIM + p : HDIM + p + 1], shape),
            )
            term = factor * part[:, at].astype(F32)
            acc = term if acc is None else acc + term
        out[:, at] = acc.astype(BF16)


def call(body, outs, name, units, *args):
    specs = [SMEM] + [VMEM] * (len(args) - 1)
    moved = sum(a.size * a.dtype.itemsize for a in args)
    moved += sum(o.size * o.dtype.itemsize for o in outs)
    return pl.pallas_call(
        body,
        out_shape=outs,
        in_specs=specs,
        out_specs=[VMEM] * len(outs),
        name=name,
        compiler_params=pltpu.CompilerParams(vmem_limit_bytes=16 << 20),
        cost_estimate=pl.CostEstimate(
            flops=units,
            transcendentals=0,
            bytes_accessed=1024,
        ),
    )(*args)


def shaped(*shape, dtype=F32):
    return jax.ShapeDtypeStruct(shape, dtype)


def on_device(query_states, key_states, value_states, tissue):
    q, k, v = (a.reshape(TOK, HD) for a in (query_states, key_states, value_states))
    rows, cols = tissue.shape
    far, near = swaps(rows, 1), swaps(rows, 0)
    beyond, beside = swaps(cols, 1), swaps(cols, 0)
    kvb = lax.ppermute(jnp.stack([k, v]), "row", far)
    qd = lax.ppermute(q, "col", beyond)
    qc = lax.ppermute(q, "col", beside)
    ka = lax.ppermute(k, "row", near)
    va = lax.ppermute(v, "row", near)
    state = [shaped(3, TOK, HD)] * 3
    top, tot, mix = call(early_kernel, state, "early", 6, tissue, q, qc, qd, k, v, ka, va)
    pack = shaped(TOK, HD + PAIR, dtype=BF16)
    out_c, out_d = call(side_kernel, [pack] * 2, "side", 2, tissue, qc, qd, kvb, top, tot, mix)
    in_d = lax.ppermute(out_d, "col", beyond)
    in_c = lax.ppermute(out_c, "col", beside)
    own = [shaped(TOK, HD), shaped(TOK, PAIR), shaped(TOK, PAIR)]
    mix, top, tot = call(own_kernel, own, "own", 1, tissue, q, kvb, top, tot, mix)
    (out,) = call(
        functools.partial(merge_kernel, cols), [shaped(TOK, HD, dtype=BF16)], "merge", 0,
        tissue, mix, top, tot, in_c, in_d,
    )
    return out.reshape(1, 1, TOK, HD)


def solution(mesh):
    return jax.shard_map(
        on_device,
        mesh=mesh,
        in_specs=(
            P("row", "col", None, None),
            P("row", "col", None, None),
            P("row", "col", None, None),
            P(),
        ),
        out_specs=P("row", "col", None, None),
        check_vma=False,
    )
```

```python
import functools

import jax
import jax.numpy as jnp
from jax import lax
from jax.experimental import pallas as pl
from jax.experimental.pallas import tpu as pltpu
from jax.sharding import PartitionSpec as P

HDIM = 64
HEADS = 12
PAIR = 2 * HDIM
PAIRS = HEADS // 2
TOK = 128
HD = HEADS * HDIM
LOG2E = 1.4426950408889634
SCALE = HDIM ** (-0.5) * LOG2E
NEG = -1e30
FLOOR = -1e20
VMEM = pl.BlockSpec(memory_space=pltpu.VMEM)
ANY = pl.BlockSpec(memory_space=pl.ANY)
SMEM = pl.BlockSpec(memory_space=pltpu.SMEM)
F32 = jnp.float32
BF16 = jnp.bfloat16


def swaps(count, first):
    pairs = []
    for i in range(first, count - 1, 2):
        pairs += [(i, i + 1), (i + 1, i)]
    return pairs


def partner(i, odd):
    return ((i + 1) ^ 1) - 1 if odd else i ^ 1


def lane_low():
    return lax.broadcasted_iota(jnp.int32, (TOK, PAIR), 1) < HDIM


def position():
    return lax.axis_index("row"), lax.axis_index("col")


def tile_bias(tissue, row, col):
    rows, cols = tissue.shape
    inside = (row >= 0) & (row < rows)
    at = tissue[jnp.clip(row, 0, rows - 1), col]
    return jnp.where(inside & (at > 0), 0.0, NEG).astype(F32)


def attend_pair(query, keys, values, biases, low):
    zero = jnp.zeros_like(query)
    both = jnp.concatenate([jnp.where(low, query, zero), jnp.where(low, zero, query)], axis=0)
    scores = []
    for key, bias in zip(keys, biases):
        s = lax.dot_general(both, key, (((1,), (1,)), ((), ())), preferred_element_type=F32) * SCALE
        scores.append(s if bias is None else s + bias)
    top = functools.reduce(jnp.maximum, scores)
    top = jnp.maximum(jnp.max(top, axis=1, keepdims=True), FLOOR)
    weights = [jnp.exp2(s - top) for s in scores]
    total = jnp.sum(functools.reduce(jnp.add, weights), axis=1, keepdims=True)
    mixed = functools.reduce(
        jnp.add,
        [jnp.dot(w.astype(BF16), v, preferred_element_type=F32) for w, v in zip(weights, values)],
    )
    shape = (TOK, PAIR)
    top2 = jnp.where(low, jnp.broadcast_to(top[:TOK], shape), jnp.broadcast_to(top[TOK:], shape))
    tot2 = jnp.where(low, jnp.broadcast_to(total[:TOK], shape), jnp.broadcast_to(total[TOK:], shape))
    mix2 = jnp.where(low, mixed[:TOK], mixed[TOK:])
    return top2, tot2, mix2


def lanes(p):
    return slice(p * PAIR, (p + 1) * PAIR)


def early_kernel(cols, tissue, q_hbm, qd, qc, k_hbm, v_hbm, kva, top_ref, tot_ref, mix_ref, flags, q, k, v, sems):
    copies = [
        pltpu.make_async_copy(source, target, sems.at[n])
        for n, (source, target) in enumerate(((q_hbm, q), (k_hbm, k), (v_hbm, v)))
    ]
    for copy in copies:
        copy.start()
    row, col = position()
    low = lane_low()
    own = tile_bias(tissue, row, col)
    near = tile_bias(tissue, partner(row, False), col)
    far = tile_bias(tissue, partner(row, True), col)
    other = partner(col, True)
    missing = jnp.where((other >= 0) & (other < cols), 0.0, NEG).astype(F32)
    shown = jnp.where(tissue[row, col] > 0, 1.0, 0.0).astype(F32)
    for n, value in enumerate((far, missing, shown)):
        flags[n : n + 1, :] = jnp.full((1, PAIR), value, F32)
    for copy in copies:
        copy.wait()
    for p in range(PAIRS):
        at = lanes(p)
        for i, query in enumerate((q, qc, qd)):
            t, l, m = attend_pair(
                query[:, at], (k[:, at], kva[:TOK, at]), (v[:, at], kva[TOK:, at]),
                (None if i == 0 else own, near), low,
            )
            top_ref[i, :, at] = t
            tot_ref[i, :, at] = l
            mix_ref[i, :, at] = m


def late_part(query, kvb, bias, top, tot, mix, i, p, low):
    at = lanes(p)
    t, l, m = attend_pair(query[:, at], (kvb[:TOK, at],), (kvb[TOK : 2 * TOK, at],), (bias,), low)
    t0 = top[i, :, at]
    best = jnp.maximum(t, t0)
    new, old = jnp.exp2(t - best), jnp.exp2(t0 - best)
    return best, l * new + tot[i, :, at] * old, m * new + mix[i, :, at] * old


def spot(p):
    return (lax.broadcasted_iota(jnp.int32, (TOK, PAIR), 1) & (HDIM - 1)) == p


def pieces(x, count):
    parts = []
    for _ in range(count):
        part = x.astype(BF16).astype(F32)
        parts.append(part)
        x = x - part
    return parts


def side_kernel(flags, qd, qc, kvb, top, tot, mix, out_d, out_c):
    low = lane_low()
    bias = flags[0:1, :]
    for i, (query, out) in enumerate(((qc, out_c), (qd, out_d))):
        stats = jnp.zeros((TOK, PAIR), F32)
        for p in range(PAIRS):
            best, total, mixed = late_part(query, kvb, bias, top, tot, mix, i + 1, p, low)
            out[:, lanes(p)] = mixed.astype(BF16)
            for slot, piece in enumerate(pieces(best, 3) + pieces(total, 2)):
                stats = jnp.where(spot(p + 8 * slot), piece, stats)
        out[:, HD:] = stats.astype(BF16)


def own_kernel(flags, q, kvb, top, tot, mix, mix_out, top_out, tot_out):
    low = lane_low()
    bias = flags[0:1, :]
    tops = jnp.zeros((TOK, PAIR), F32)
    tots = jnp.ones((TOK, PAIR), F32)
    for p in range(PAIRS):
        best, total, mixed = late_part(q, kvb, bias, top, tot, mix, 0, p, low)
        mix_out[:, lanes(p)] = mixed
        tops = jnp.where(spot(p), best, tops)
        tots = jnp.where(spot(p), total, tots)
    top_out[...] = tops
    tot_out[...] = tots


def merge_kernel(flags, mix, top, tot, in_d, in_c, out):
    low = lane_low()
    missing, own = flags[1:2, :], flags[2:3, :]
    tops, tots = [top[...]], [tot[...]]
    for part, gap in ((in_c, None), (in_d, missing)):
        stats = part[:, HD:].astype(F32)
        slots = [stats] + [pltpu.roll(stats, PAIR - 8 * slot, 1) for slot in range(1, 5)]
        highest = slots[0] + slots[1] + slots[2]
        tops.append(highest if gap is None else highest + gap)
        tots.append(slots[3] + slots[4])
    best = functools.reduce(jnp.maximum, tops)
    shares = [jnp.exp2(t - best) for t in tops]
    total = functools.reduce(jnp.add, [s * t for s, t in zip(shares, tots)])
    shares = [s * own / total for s in shares]
    for p in range(PAIRS):
        at = lanes(p)
        acc = None
        for share, part in zip(shares, (mix, in_c, in_d)):
            shape = (TOK, PAIR)
            factor = jnp.where(
                low,
                jnp.broadcast_to(share[:, p : p + 1], shape),
                jnp.broadcast_to(share[:, HDIM + p : HDIM + p + 1], shape),
            )
            term = factor * part[:, at].astype(F32)
            acc = term if acc is None else acc + term
        out[:, at] = acc.astype(BF16)


def call(body, outs, name, specs, *args, scratch=()):
    return pl.pallas_call(
        body,
        out_shape=outs,
        in_specs=specs,
        out_specs=[VMEM] * len(outs),
        scratch_shapes=scratch,
        name=name,
        compiler_params=pltpu.CompilerParams(vmem_limit_bytes=16 << 20),
        cost_estimate=pl.CostEstimate(flops=1, transcendentals=0, bytes_accessed=1024),
    )(*args)


def shaped(*shape, dtype=F32):
    return jax.ShapeDtypeStruct(shape, dtype)


def on_device(query_states, key_states, value_states, tissue):
    q, k, v = (a.reshape(TOK, HD) for a in (query_states, key_states, value_states))
    rows, cols = tissue.shape
    far, near = swaps(rows, 1), swaps(rows, 0)
    beyond, beside = swaps(cols, 1), swaps(cols, 0)
    kvb = lax.ppermute(jnp.concatenate([k, v, jnp.zeros((8, HD), BF16)]), "row", far)
    kva = lax.ppermute(jnp.concatenate([k, v]), "row", near)
    qd = lax.ppermute(q, "col", beyond)
    qc = lax.ppermute(q, "col", beside)
    outs = [shaped(3, TOK, HD)] * 3 + [shaped(8, PAIR)]
    staged = [pltpu.VMEM((TOK, HD), BF16)] * 3 + [pltpu.SemaphoreType.DMA((3,))]
    top, tot, mix, flags = call(
        functools.partial(early_kernel, cols), outs, "early", [SMEM, ANY, VMEM, VMEM, ANY, ANY, VMEM],
        tissue, q, qd, qc, k, v, kva, scratch=staged,
    )
    pack = shaped(TOK, HD + PAIR, dtype=BF16)
    out_d, out_c = call(side_kernel, [pack] * 2, "side", [VMEM] * 7, flags, qd, qc, kvb, top, tot, mix)
    in_d = lax.ppermute(out_d, "col", beyond)
    in_c = lax.ppermute(out_c, "col", beside)
    own = [shaped(TOK, HD), shaped(TOK, PAIR), shaped(TOK, PAIR)]
    mix, top, tot = call(own_kernel, own, "own", [VMEM] * 6, flags, q, kvb, top, tot, mix)
    (out,) = call(
        merge_kernel, [shaped(TOK, HD, dtype=BF16)], "merge", [VMEM] * 6, flags, mix, top, tot, in_d, in_c
    )
    return out.reshape(1, 1, TOK, HD)


def solution(mesh):
    return jax.shard_map(
        on_device,
        mesh=mesh,
        in_specs=(
            P("row", "col", None, None),
            P("row", "col", None, None),
            P("row", "col", None, None),
            P(),
        ),
        out_specs=P("row", "col", None, None),
        check_vma=False,
    )
```

```python
import functools

import jax
import jax.numpy as jnp
from jax import lax
from jax.experimental import pallas as pl
from jax.experimental.pallas import tpu as pltpu
from jax.sharding import PartitionSpec as P

HDIM = 64
HEADS = 12
PAIR = 2 * HDIM
PAIRS = HEADS // 2
TOK = 128
HD = HEADS * HDIM
LOG2E = 1.4426950408889634
SCALE = HDIM ** (-0.5) * LOG2E
NEG = -1e30
FLOOR = -1e20
VMEM = pl.BlockSpec(memory_space=pltpu.VMEM)
ANY = pl.BlockSpec(memory_space=pl.ANY)
SMEM = pl.BlockSpec(memory_space=pltpu.SMEM)
F32 = jnp.float32
BF16 = jnp.bfloat16


def swaps(count, first):
    pairs = []
    for i in range(first, count - 1, 2):
        pairs += [(i, i + 1), (i + 1, i)]
    return pairs


def partner(i, odd):
    return ((i + 1) ^ 1) - 1 if odd else i ^ 1


def lane_low():
    return lax.broadcasted_iota(jnp.int32, (TOK, PAIR), 1) < HDIM


def position():
    return lax.axis_index("row"), lax.axis_index("col")


def tile_bias(tissue, row, col):
    rows, cols = tissue.shape
    inside = (row >= 0) & (row < rows)
    at = tissue[jnp.clip(row, 0, rows - 1), col]
    return jnp.where(inside & (at > 0), 0.0, NEG).astype(F32)


def attend_pair(query, keys, values, biases, low):
    zero = jnp.zeros_like(query)
    both = jnp.concatenate([jnp.where(low, query, zero), jnp.where(low, zero, query)], axis=0)
    scores = []
    for key, bias in zip(keys, biases):
        s = lax.dot_general(both, key, (((1,), (1,)), ((), ())), preferred_element_type=F32) * SCALE
        scores.append(s if bias is None else s + bias)
    top = functools.reduce(jnp.maximum, scores)
    top = jnp.maximum(jnp.max(top, axis=1, keepdims=True), FLOOR)
    weights = [jnp.exp2(s - top) for s in scores]
    total = jnp.sum(functools.reduce(jnp.add, weights), axis=1, keepdims=True)
    mixed = functools.reduce(
        jnp.add,
        [jnp.dot(w.astype(BF16), v, preferred_element_type=F32) for w, v in zip(weights, values)],
    )
    shape = (TOK, PAIR)
    top2 = jnp.where(low, jnp.broadcast_to(top[:TOK], shape), jnp.broadcast_to(top[TOK:], shape))
    tot2 = jnp.where(low, jnp.broadcast_to(total[:TOK], shape), jnp.broadcast_to(total[TOK:], shape))
    mix2 = jnp.where(low, mixed[:TOK], mixed[TOK:])
    return top2, tot2, mix2


def lanes(p):
    return slice(p * PAIR, (p + 1) * PAIR)


def own_tile(query, kv, bias, i, low, top_ref, tot_ref, mix_ref):
    for p in range(PAIRS):
        at = lanes(p)
        t, l, m = attend_pair(query[:, at], (kv[:TOK, at],), (kv[TOK:, at],), (bias,), low)
        top_ref[i, :, at] = t
        tot_ref[i, :, at] = l
        mix_ref[i, :, at] = m


def early_kernel(cols, tissue, q, kv, top_ref, tot_ref, mix_ref, flags):
    row, col = position()
    low = lane_low()
    own = tile_bias(tissue, row, col)
    near = tile_bias(tissue, partner(row, False), col)
    far = tile_bias(tissue, partner(row, True), col)
    other = partner(col, True)
    missing = jnp.where((other >= 0) & (other < cols), 0.0, NEG).astype(F32)
    shown = jnp.where(tissue[row, col] > 0, 1.0, 0.0).astype(F32)
    for n, value in enumerate((near, far, missing, shown, own)):
        flags[n : n + 1, :] = jnp.full((1, PAIR), value, F32)
    own_tile(q, kv, None, 0, low, top_ref, tot_ref, mix_ref)


def neighbour_kernel(flags, qc, qd, kv, top_ref, tot_ref, mix_ref):
    low = lane_low()
    own_tile(qd, kv, flags[4:5, :], 0, low, top_ref, tot_ref, mix_ref)
    own_tile(qc, kv, flags[4:5, :], 1, low, top_ref, tot_ref, mix_ref)


def late_part(query, kva, kvb, flags, state, i, p, low):
    at = lanes(p)
    t, l, m = attend_pair(
        query[:, at], (kva[:TOK, at], kvb[:TOK, at]), (kva[TOK:, at], kvb[TOK:, at]),
        (flags[0:1, :], flags[1:2, :]), low,
    )
    top, tot, mix = state
    t0 = top[i, :, at]
    best = jnp.maximum(t, t0)
    new, old = jnp.exp2(t - best), jnp.exp2(t0 - best)
    return best, l * new + tot[i, :, at] * old, m * new + mix[i, :, at] * old


def spot(p):
    return (lax.broadcasted_iota(jnp.int32, (TOK, PAIR), 1) & (HDIM - 1)) == p


def pieces(x, count):
    parts = []
    for _ in range(count):
        part = x.astype(BF16).astype(F32)
        parts.append(part)
        x = x - part
    return parts


def side_kernel(flags, qc, qd, kva, kvb, top, tot, mix, out_d, out_c):
    low = lane_low()
    for i, (query, out) in enumerate(((qd, out_d), (qc, out_c))):
        stats = jnp.zeros((TOK, PAIR), F32)
        for p in range(PAIRS):
            best, total, mixed = late_part(query, kva, kvb, flags, (top, tot, mix), i, p, low)
            out[:, lanes(p)] = mixed.astype(BF16)
            for slot, piece in enumerate(pieces(best, 3) + pieces(total, 2)):
                stats = jnp.where(spot(p + 8 * slot), piece, stats)
        out[:, HD:] = stats.astype(BF16)


def own_kernel(flags, q, kva, kvb, top, tot, mix, mix_out, top_out, tot_out):
    low = lane_low()
    tops = jnp.zeros((TOK, PAIR), F32)
    tots = jnp.ones((TOK, PAIR), F32)
    for p in range(PAIRS):
        best, total, mixed = late_part(q, kva, kvb, flags, (top, tot, mix), 0, p, low)
        mix_out[:, lanes(p)] = mixed
        tops = jnp.where(spot(p), best, tops)
        tots = jnp.where(spot(p), total, tots)
    top_out[...] = tops
    tot_out[...] = tots


def merge_kernel(flags, mix, top, tot, in_d, in_c, out):
    low = lane_low()
    missing, own = flags[2:3, :], flags[3:4, :]
    tops, tots = [top[...]], [tot[...]]
    for part, gap in ((in_c, None), (in_d, missing)):
        stats = part[:, HD:].astype(F32)
        slots = [stats] + [pltpu.roll(stats, PAIR - 8 * slot, 1) for slot in range(1, 5)]
        highest = slots[0] + slots[1] + slots[2]
        tops.append(highest if gap is None else highest + gap)
        tots.append(slots[3] + slots[4])
    best = functools.reduce(jnp.maximum, tops)
    shares = [jnp.exp2(t - best) for t in tops]
    total = functools.reduce(jnp.add, [s * t for s, t in zip(shares, tots)])
    shares = [s * own / total for s in shares]
    for p in range(PAIRS):
        at = lanes(p)
        acc = None
        for share, part in zip(shares, (mix, in_c, in_d)):
            shape = (TOK, PAIR)
            factor = jnp.where(
                low,
                jnp.broadcast_to(share[:, p : p + 1], shape),
                jnp.broadcast_to(share[:, HDIM + p : HDIM + p + 1], shape),
            )
            term = factor * part[:, at].astype(F32)
            acc = term if acc is None else acc + term
        out[:, at] = acc.astype(BF16)


def call(body, outs, name, specs, *args, scratch=()):
    return pl.pallas_call(
        body,
        out_shape=outs,
        in_specs=specs,
        out_specs=[VMEM] * len(outs),
        scratch_shapes=scratch,
        name=name,
        compiler_params=pltpu.CompilerParams(vmem_limit_bytes=16 << 20),
        cost_estimate=pl.CostEstimate(flops=1, transcendentals=0, bytes_accessed=1024),
    )(*args)


def shaped(*shape, dtype=F32):
    return jax.ShapeDtypeStruct(shape, dtype)


def on_device(query_states, key_states, value_states, tissue):
    q, k, v = (a.reshape(TOK, HD) for a in (query_states, key_states, value_states))
    rows, cols = tissue.shape
    far, near = swaps(rows, 1), swaps(rows, 0)
    beyond, beside = swaps(cols, 1), swaps(cols, 0)
    stack = jnp.concatenate([k, v])
    kvb = lax.ppermute(stack, "row", far)
    kva = lax.ppermute(stack, "row", near)
    qd = lax.ppermute(q, "col", beyond)
    qc = lax.ppermute(q, "col", beside)
    outs = [shaped(1, TOK, HD)] * 3
    *state, flags = call(
        functools.partial(early_kernel, cols), outs + [shaped(8, PAIR)], "early", [SMEM, VMEM, VMEM],
        tissue, q, stack,
    )
    outs = [shaped(2, TOK, HD)] * 3
    side_state = call(neighbour_kernel, outs, "neighbour", [VMEM] * 4, flags, qc, qd, stack)
    pack = shaped(TOK, HD + PAIR, dtype=BF16)
    out_d, out_c = call(
        side_kernel, [pack] * 2, "side", [VMEM] * 8, flags, qc, qd, kva, kvb, *side_state
    )
    in_d = lax.ppermute(out_d, "col", beyond)
    in_c = lax.ppermute(out_c, "col", beside)
    own = [shaped(TOK, HD), shaped(TOK, PAIR), shaped(TOK, PAIR)]
    mix, top, tot = call(own_kernel, own, "own", [VMEM] * 7, flags, q, kva, kvb, *state)
    (out,) = call(
        merge_kernel, [shaped(TOK, HD, dtype=BF16)], "merge", [VMEM] * 6, flags, mix, top, tot, in_d, in_c
    )
    return out.reshape(1, 1, TOK, HD)


def solution(mesh):
    return jax.shard_map(
        on_device,
        mesh=mesh,
        in_specs=(
            P("row", "col", None, None),
            P("row", "col", None, None),
            P("row", "col", None, None),
            P(),
        ),
        out_specs=P("row", "col", None, None),
        check_vma=False,
    )
```

```python
import functools

import jax
import jax.numpy as jnp
from jax import lax
from jax.experimental import pallas as pl
from jax.experimental.pallas import tpu as pltpu
from jax.sharding import PartitionSpec as P

HDIM = 64
HEADS = 12
PAIR = 2 * HDIM
PAIRS = HEADS // 2
TOK = 128
HD = HEADS * HDIM
LOG2E = 1.4426950408889634
SCALE = HDIM ** (-0.5) * LOG2E
NEG = -1e30
FLOOR = -1e20
VMEM = pl.BlockSpec(memory_space=pltpu.VMEM)
ANY = pl.BlockSpec(memory_space=pl.ANY)
SMEM = pl.BlockSpec(memory_space=pltpu.SMEM)
F32 = jnp.float32
BF16 = jnp.bfloat16


def swaps(count, first):
    pairs = []
    for i in range(first, count - 1, 2):
        pairs += [(i, i + 1), (i + 1, i)]
    return pairs


def partner(i, odd):
    return ((i + 1) ^ 1) - 1 if odd else i ^ 1


def lane_low():
    return lax.broadcasted_iota(jnp.int32, (TOK, PAIR), 1) < HDIM


def position():
    return lax.axis_index("row"), lax.axis_index("col")


def tile_bias(tissue, row, col):
    rows, cols = tissue.shape
    inside = (row >= 0) & (row < rows)
    at = tissue[jnp.clip(row, 0, rows - 1), col]
    return jnp.where(inside & (at > 0), 0.0, NEG).astype(F32)


def attend_pair(query, keys, values, biases, low):
    zero = jnp.zeros_like(query)
    both = jnp.concatenate([jnp.where(low, query, zero), jnp.where(low, zero, query)], axis=0)
    scores = []
    for key, bias in zip(keys, biases):
        s = lax.dot_general(both, key, (((1,), (1,)), ((), ())), preferred_element_type=F32) * SCALE
        scores.append(s if bias is None else s + bias)
    top = functools.reduce(jnp.maximum, scores)
    top = jnp.maximum(jnp.max(top, axis=1, keepdims=True), FLOOR)
    weights = [jnp.exp2(s - top) for s in scores]
    total = jnp.sum(functools.reduce(jnp.add, weights), axis=1, keepdims=True)
    mixed = functools.reduce(
        jnp.add,
        [jnp.dot(w.astype(BF16), v, preferred_element_type=F32) for w, v in zip(weights, values)],
    )
    shape = (TOK, PAIR)
    top2 = jnp.where(low, jnp.broadcast_to(top[:TOK], shape), jnp.broadcast_to(top[TOK:], shape))
    tot2 = jnp.where(low, jnp.broadcast_to(total[:TOK], shape), jnp.broadcast_to(total[TOK:], shape))
    mix2 = jnp.where(low, mixed[:TOK], mixed[TOK:])
    return top2, tot2, mix2


def attend_late(query, kva, kvb, flags, at, low):
    zero = jnp.zeros_like(query)
    both = jnp.concatenate([jnp.where(low, query, zero), jnp.where(low, zero, query)], axis=0)
    keys = jnp.concatenate([kva[:TOK, at], kvb[:TOK, at]], axis=0)
    values = jnp.concatenate([kva[TOK:, at], kvb[TOK:, at]], axis=0)
    values = jnp.concatenate([values, jnp.ones_like(values)], axis=1)
    scores = lax.dot_general(both, keys, (((1,), (1,)), ((), ())), preferred_element_type=F32) * SCALE
    scores = scores + jnp.concatenate([flags[0:1, :], flags[1:2, :]], axis=1)
    top = jnp.maximum(jnp.max(scores, axis=1, keepdims=True), FLOOR)
    mixed = jnp.dot(jnp.exp2(scores - top).astype(BF16), values, preferred_element_type=F32)
    shape = (TOK, PAIR)
    top2 = jnp.where(low, jnp.broadcast_to(top[:TOK], shape), jnp.broadcast_to(top[TOK:], shape))
    tot2 = jnp.where(low, mixed[:TOK, PAIR:], mixed[TOK:, PAIR:])
    mix2 = jnp.where(low, mixed[:TOK, :PAIR], mixed[TOK:, :PAIR])
    return top2, tot2, mix2


def lanes(p):
    return slice(p * PAIR, (p + 1) * PAIR)


def own_tile(query, kv, bias, i, low, top_ref, tot_ref, mix_ref):
    for p in range(PAIRS):
        at = lanes(p)
        t, l, m = attend_pair(query[:, at], (kv[:TOK, at],), (kv[TOK:, at],), (bias,), low)
        top_ref[i, :, at] = t
        tot_ref[i, :, at] = l
        mix_ref[i, :, at] = m


def early_kernel(cols, tissue, q, kv, top_ref, tot_ref, mix_ref, flags):
    row, col = position()
    low = lane_low()
    own = tile_bias(tissue, row, col)
    near = tile_bias(tissue, partner(row, False), col)
    far = tile_bias(tissue, partner(row, True), col)
    other = partner(col, True)
    missing = jnp.where((other >= 0) & (other < cols), 0.0, NEG).astype(F32)
    shown = jnp.where(tissue[row, col] > 0, 1.0, 0.0).astype(F32)
    for n, value in enumerate((near, far, missing, shown, own)):
        flags[n : n + 1, :] = jnp.full((1, PAIR), value, F32)
    own_tile(q, kv, None, 0, low, top_ref, tot_ref, mix_ref)


def neighbour_kernel(flags, qc, qd, kv, top_ref, tot_ref, mix_ref):
    low = lane_low()
    own_tile(qd, kv, flags[4:5, :], 0, low, top_ref, tot_ref, mix_ref)
    own_tile(qc, kv, flags[4:5, :], 1, low, top_ref, tot_ref, mix_ref)


def late_part(query, kva, kvb, flags, state, i, p, low):
    at = lanes(p)
    t, l, m = attend_late(query[:, at], kva, kvb, flags, at, low)
    top, tot, mix = state
    t0 = top[i, :, at]
    best = jnp.maximum(t, t0)
    new, old = jnp.exp2(t - best), jnp.exp2(t0 - best)
    return best, l * new + tot[i, :, at] * old, m * new + mix[i, :, at] * old


def spot(p):
    return (lax.broadcasted_iota(jnp.int32, (TOK, PAIR), 1) & (HDIM - 1)) == p


def pieces(x, count):
    parts = []
    for _ in range(count):
        part = x.astype(BF16).astype(F32)
        parts.append(part)
        x = x - part
    return parts


def side_kernel(flags, qc, qd, kva, kvb, top, tot, mix, out_d, out_c):
    low = lane_low()
    for i, (query, out) in enumerate(((qd, out_d), (qc, out_c))):
        tops = jnp.zeros((TOK, PAIR), F32)
        tots = jnp.zeros((TOK, PAIR), F32)
        for p in range(PAIRS):
            best, total, mixed = late_part(query, kva, kvb, flags, (top, tot, mix), i, p, low)
            out[:, lanes(p)] = mixed.astype(BF16)
            tops = jnp.where(spot(p), best, tops)
            tots = jnp.where(spot(p), total, tots)
        stats = jnp.zeros((TOK, PAIR), F32)
        for slot, piece in enumerate(pieces(tops, 3) + pieces(tots, 2)):
            stats = stats + (pltpu.roll(piece, 8 * slot, 1) if slot else piece)
        out[:, HD:] = stats.astype(BF16)


def own_kernel(flags, q, kva, kvb, top, tot, mix, mix_out, top_out, tot_out):
    low = lane_low()
    tops = jnp.zeros((TOK, PAIR), F32)
    tots = jnp.ones((TOK, PAIR), F32)
    for p in range(PAIRS):
        best, total, mixed = late_part(q, kva, kvb, flags, (top, tot, mix), 0, p, low)
        mix_out[:, lanes(p)] = mixed
        tops = jnp.where(spot(p), best, tops)
        tots = jnp.where(spot(p), total, tots)
    top_out[...] = tops
    tot_out[...] = tots


def merge_kernel(flags, mix, top, tot, in_d, in_c, out):
    low = lane_low()
    missing, own = flags[2:3, :], flags[3:4, :]
    tops, tots = [top[...]], [tot[...]]
    for part, gap in ((in_c, None), (in_d, missing)):
        stats = part[:, HD:].astype(F32)
        slots = [stats] + [pltpu.roll(stats, PAIR - 8 * slot, 1) for slot in range(1, 5)]
        highest = slots[0] + slots[1] + slots[2]
        tops.append(highest if gap is None else highest + gap)
        tots.append(slots[3] + slots[4])
    best = functools.reduce(jnp.maximum, tops)
    shares = [jnp.exp2(t - best) for t in tops]
    total = functools.reduce(jnp.add, [s * t for s, t in zip(shares, tots)])
    keep = (lax.broadcasted_iota(jnp.int32, (TOK, PAIR), 1) & (HDIM - 1)) < PAIRS
    shares = [jnp.where(keep, s * own / total, 0.0) for s in shares]
    source = lax.broadcasted_iota(jnp.int32, (PAIR, HD), 0)
    target = lax.broadcasted_iota(jnp.int32, (PAIR, HD), 1)
    pick = (source == (target // PAIR + (target & HDIM))).astype(BF16)
    pick = jnp.concatenate([pick, pick], axis=0)
    spread = [
        jnp.dot(jnp.concatenate(pieces(s, 2), axis=1).astype(BF16), pick, preferred_element_type=F32) for s in shares
    ]
    for p in range(PAIRS):
        at = lanes(p)
        acc = None
        for factors, part in zip(spread, (mix, in_c, in_d)):
            term = factors[:, at] * part[:, at].astype(F32)
            acc = term if acc is None else acc + term
        out[:, at] = acc.astype(BF16)


def call(body, outs, name, specs, *args, scratch=()):
    return pl.pallas_call(
        body,
        out_shape=outs,
        in_specs=specs,
        out_specs=[VMEM] * len(outs),
        scratch_shapes=scratch,
        name=name,
        compiler_params=pltpu.CompilerParams(vmem_limit_bytes=16 << 20),
        cost_estimate=pl.CostEstimate(flops=1, transcendentals=0, bytes_accessed=1024),
    )(*args)


def shaped(*shape, dtype=F32):
    return jax.ShapeDtypeStruct(shape, dtype)


def on_device(query_states, key_states, value_states, tissue):
    q, k, v = (a.reshape(TOK, HD) for a in (query_states, key_states, value_states))
    rows, cols = tissue.shape
    far, near = swaps(rows, 1), swaps(rows, 0)
    beyond, beside = swaps(cols, 1), swaps(cols, 0)
    stack = jnp.concatenate([k, v])
    kvb = lax.ppermute(stack, "row", far)
    kva = lax.ppermute(stack, "row", near)
    qd = lax.ppermute(q, "col", beyond)
    qc = lax.ppermute(q, "col", beside)
    outs = [shaped(1, TOK, HD)] * 3
    *state, flags = call(
        functools.partial(early_kernel, cols), outs + [shaped(8, PAIR)], "early", [SMEM, VMEM, VMEM],
        tissue, q, stack,
    )
    outs = [shaped(2, TOK, HD)] * 3
    side_state = call(neighbour_kernel, outs, "neighbour", [VMEM] * 4, flags, qc, qd, stack)
    pack = shaped(TOK, HD + PAIR, dtype=BF16)
    out_d, out_c = call(
        side_kernel, [pack] * 2, "side", [VMEM] * 8, flags, qc, qd, kva, kvb, *side_state
    )
    in_d = lax.ppermute(out_d, "col", beyond)
    in_c = lax.ppermute(out_c, "col", beside)
    own = [shaped(TOK, HD), shaped(TOK, PAIR), shaped(TOK, PAIR)]
    mix, top, tot = call(own_kernel, own, "own", [VMEM] * 7, flags, q, kva, kvb, *state)
    (out,) = call(
        merge_kernel, [shaped(TOK, HD, dtype=BF16)], "merge", [VMEM] * 6, flags, mix, top, tot, in_d, in_c
    )
    return out.reshape(1, 1, TOK, HD)


def solution(mesh):
    return jax.shard_map(
        on_device,
        mesh=mesh,
        in_specs=(
            P("row", "col", None, None),
            P("row", "col", None, None),
            P("row", "col", None, None),
            P(),
        ),
        out_specs=P("row", "col", None, None),
        check_vma=False,
    )
```

```python
import functools

import jax
import jax.numpy as jnp
from jax import lax
from jax.experimental import pallas as pl
from jax.experimental.pallas import tpu as pltpu
from jax.sharding import PartitionSpec as P

HDIM = 64
HEADS = 12
PAIR = 2 * HDIM
PAIRS = HEADS // 2
TOK = 128
HD = HEADS * HDIM
LOG2E = 1.4426950408889634
SCALE = HDIM ** (-0.5) * LOG2E
NEG = -1e30
FLOOR = -1e20
VMEM = pl.BlockSpec(memory_space=pltpu.VMEM)
ANY = pl.BlockSpec(memory_space=pl.ANY)
SMEM = pl.BlockSpec(memory_space=pltpu.SMEM)
F32 = jnp.float32
BF16 = jnp.bfloat16


def swaps(count, first):
    pairs = []
    for i in range(first, count - 1, 2):
        pairs += [(i, i + 1), (i + 1, i)]
    return pairs


def partner(i, odd):
    return ((i + 1) ^ 1) - 1 if odd else i ^ 1


def lane_low():
    return lax.broadcasted_iota(jnp.int32, (TOK, PAIR), 1) < HDIM


def position():
    return lax.axis_index("row"), lax.axis_index("col")


def tile_bias(tissue, row, col):
    rows, cols = tissue.shape
    inside = (row >= 0) & (row < rows)
    at = tissue[jnp.clip(row, 0, rows - 1), col]
    return jnp.where(inside & (at > 0), 0.0, NEG).astype(F32)


def attend_pair(query, keys, values, biases, low):
    zero = jnp.zeros_like(query)
    both = jnp.concatenate([jnp.where(low, query, zero), jnp.where(low, zero, query)], axis=0)
    scores = []
    for key, bias in zip(keys, biases):
        s = lax.dot_general(both, key, (((1,), (1,)), ((), ())), preferred_element_type=F32) * SCALE
        scores.append(s if bias is None else s + bias)
    top = functools.reduce(jnp.maximum, scores)
    top = jnp.maximum(jnp.max(top, axis=1, keepdims=True), FLOOR)
    weights = [jnp.exp2(s - top) for s in scores]
    total = jnp.sum(functools.reduce(jnp.add, weights), axis=1, keepdims=True)
    mixed = functools.reduce(
        jnp.add,
        [jnp.dot(w.astype(BF16), v, preferred_element_type=F32) for w, v in zip(weights, values)],
    )
    shape = (TOK, PAIR)
    top2 = jnp.where(low, jnp.broadcast_to(top[:TOK], shape), jnp.broadcast_to(top[TOK:], shape))
    tot2 = jnp.where(low, jnp.broadcast_to(total[:TOK], shape), jnp.broadcast_to(total[TOK:], shape))
    mix2 = jnp.where(low, mixed[:TOK], mixed[TOK:])
    return top2, tot2, mix2


def attend_late(query, kva, kvb, flags, at, low):
    zero = jnp.zeros_like(query)
    both = jnp.concatenate([jnp.where(low, query, zero), jnp.where(low, zero, query)], axis=0)
    keys = jnp.concatenate([kva[:TOK, at], kvb[:TOK, at]], axis=0)
    values = jnp.concatenate([kva[TOK:, at], kvb[TOK:, at]], axis=0)
    values = jnp.concatenate([values, jnp.ones_like(values)], axis=1)
    scores = lax.dot_general(both, keys, (((1,), (1,)), ((), ())), preferred_element_type=F32) * SCALE
    scores = scores + jnp.concatenate([flags[0:1, :], flags[1:2, :]], axis=1)
    top = jnp.maximum(jnp.max(scores, axis=1, keepdims=True), FLOOR)
    mixed = jnp.dot(jnp.exp2(scores - top).astype(BF16), values, preferred_element_type=F32)
    shape = (TOK, PAIR)
    top2 = jnp.where(low, jnp.broadcast_to(top[:TOK], shape), jnp.broadcast_to(top[TOK:], shape))
    tot2 = jnp.where(low, mixed[:TOK, PAIR:], mixed[TOK:, PAIR:])
    mix2 = jnp.where(low, mixed[:TOK, :PAIR], mixed[TOK:, :PAIR])
    return top2, tot2, mix2


def lanes(p):
    return slice(p * PAIR, (p + 1) * PAIR)


def own_tile(query, kv, bias, i, low, top_ref, tot_ref, mix_ref):
    for p in range(PAIRS):
        at = lanes(p)
        t, l, m = attend_pair(query[:, at], (kv[:TOK, at],), (kv[TOK:, at],), (bias,), low)
        top_ref[i, :, at] = t
        tot_ref[i, :, at] = l
        mix_ref[i, :, at] = m


def early_kernel(cols, tissue, q, kv, top_ref, tot_ref, mix_ref, flags):
    row, col = position()
    low = lane_low()
    own = tile_bias(tissue, row, col)
    near = tile_bias(tissue, partner(row, False), col)
    far = tile_bias(tissue, partner(row, True), col)
    other = partner(col, True)
    missing = jnp.where((other >= 0) & (other < cols), 0.0, NEG).astype(F32)
    shown = jnp.where(tissue[row, col] > 0, 1.0, 0.0).astype(F32)
    for n, value in enumerate((near, far, missing, shown, own)):
        flags[n : n + 1, :] = jnp.full((1, PAIR), value, F32)
    own_tile(q, kv, None, 0, low, top_ref, tot_ref, mix_ref)


def neighbour_kernel(flags, query, kv, *refs):
    own_tile(query, kv, flags[4:5, :], 0, lane_low(), *refs[-3:])


def late_part(query, kva, kvb, flags, state, i, p, low):
    at = lanes(p)
    t, l, m = attend_late(query[:, at], kva, kvb, flags, at, low)
    top, tot, mix = state
    t0 = top[i, :, at]
    best = jnp.maximum(t, t0)
    new, old = jnp.exp2(t - best), jnp.exp2(t0 - best)
    return best, l * new + tot[i, :, at] * old, m * new + mix[i, :, at] * old


def spot(p):
    return (lax.broadcasted_iota(jnp.int32, (TOK, PAIR), 1) & (HDIM - 1)) == p


def pieces(x, count):
    parts = []
    for _ in range(count):
        part = x.astype(BF16).astype(F32)
        parts.append(part)
        x = x - part
    return parts


def side_kernel(flags, query, kva, kvb, top, tot, mix, out):
    low = lane_low()
    tops = jnp.zeros((TOK, PAIR), F32)
    tots = jnp.zeros((TOK, PAIR), F32)
    for p in range(PAIRS):
        best, total, mixed = late_part(query, kva, kvb, flags, (top, tot, mix), 0, p, low)
        out[:TOK, lanes(p)] = mixed.astype(BF16)
        tops = jnp.where(spot(p), best, tops)
        tots = jnp.where(spot(p), total, tots)
    stats = jnp.zeros((TOK, PAIR), F32)
    for slot, piece in enumerate(pieces(tops, 3) + pieces(tots, 2)):
        stats = stats + (pltpu.roll(piece, 8 * slot, 1) if slot else piece)
    out[:TOK, HD:] = stats.astype(BF16)
    if out.shape[0] > TOK:
        out[TOK:, :] = jnp.zeros((out.shape[0] - TOK, HD + PAIR), BF16)


def own_kernel(flags, q, kva, kvb, top, tot, mix, mix_out, top_out, tot_out):
    low = lane_low()
    tops = jnp.zeros((TOK, PAIR), F32)
    tots = jnp.ones((TOK, PAIR), F32)
    for p in range(PAIRS):
        best, total, mixed = late_part(q, kva, kvb, flags, (top, tot, mix), 0, p, low)
        mix_out[:, lanes(p)] = mixed
        tops = jnp.where(spot(p), best, tops)
        tots = jnp.where(spot(p), total, tots)
    top_out[...] = tops
    tot_out[...] = tots


def merge_kernel(flags, mix, top, tot, in_d, in_c, out):
    low = lane_low()
    missing, own = flags[2:3, :], flags[3:4, :]
    tops, tots = [top[...]], [tot[...]]
    for part, gap in ((in_c, None), (in_d, missing)):
        stats = part[:TOK, HD:].astype(F32)
        slots = [stats] + [pltpu.roll(stats, PAIR - 8 * slot, 1) for slot in range(1, 5)]
        highest = slots[0] + slots[1] + slots[2]
        tops.append(highest if gap is None else highest + gap)
        tots.append(slots[3] + slots[4])
    best = functools.reduce(jnp.maximum, tops)
    shares = [jnp.exp2(t - best) for t in tops]
    total = functools.reduce(jnp.add, [s * t for s, t in zip(shares, tots)])
    keep = (lax.broadcasted_iota(jnp.int32, (TOK, PAIR), 1) & (HDIM - 1)) < PAIRS
    shares = [jnp.where(keep, s * own / total, 0.0) for s in shares]
    source = lax.broadcasted_iota(jnp.int32, (PAIR, HD), 0)
    target = lax.broadcasted_iota(jnp.int32, (PAIR, HD), 1)
    pick = (source == (target // PAIR + (target & HDIM))).astype(BF16)
    pick = jnp.concatenate([pick, pick], axis=0)
    spread = [
        jnp.dot(jnp.concatenate(pieces(s, 2), axis=1).astype(BF16), pick, preferred_element_type=F32) for s in shares
    ]
    for p in range(PAIRS):
        at = lanes(p)
        acc = None
        for factors, part in zip(spread, (mix, in_c, in_d)):
            term = factors[:, at] * part[:TOK, at].astype(F32)
            acc = term if acc is None else acc + term
        out[:, at] = acc.astype(BF16)


def call(body, outs, name, specs, *args, scratch=()):
    return pl.pallas_call(
        body,
        out_shape=outs,
        in_specs=specs,
        out_specs=[VMEM] * len(outs),
        scratch_shapes=scratch,
        name=name,
        compiler_params=pltpu.CompilerParams(vmem_limit_bytes=16 << 20),
        cost_estimate=pl.CostEstimate(flops=1, transcendentals=0, bytes_accessed=1024),
    )(*args)


def shaped(*shape, dtype=F32):
    return jax.ShapeDtypeStruct(shape, dtype)


def on_device(query_states, key_states, value_states, tissue):
    q, k, v = (a.reshape(TOK, HD) for a in (query_states, key_states, value_states))
    rows, cols = tissue.shape
    far, near = swaps(rows, 1), swaps(rows, 0)
    beyond, beside = swaps(cols, 1), swaps(cols, 0)
    stack = jnp.concatenate([k, v])
    kvb = lax.ppermute(stack, "row", far)
    kva = lax.ppermute(stack, "row", near)
    qd = lax.ppermute(q, "col", beyond)
    qc = lax.ppermute(q, "col", beside)
    outs = [shaped(1, TOK, HD)] * 3
    *state, flags = call(
        functools.partial(early_kernel, cols), outs + [shaped(8, PAIR)], "early", [SMEM, VMEM, VMEM],
        tissue, q, stack,
    )
    state_c = call(neighbour_kernel, outs, "neighbour", [VMEM] * 3, flags, qc, stack)
    state_d = call(neighbour_kernel, outs, "neighbour", [VMEM] * 3 + [ANY], flags, qd, stack, state_c[0])
    pack = shaped(TOK, HD + PAIR, dtype=BF16)
    pack_d = shaped(TOK + 8, HD + PAIR, dtype=BF16)
    (out_d,) = call(side_kernel, [pack_d], "beyond", [VMEM] * 7, flags, qd, kva, kvb, *state_d)
    in_d = lax.ppermute(out_d, "col", beyond)
    (out_c,) = call(side_kernel, [pack], "beside", [VMEM] * 7, flags, qc, kva, kvb, *state_c)
    in_c = lax.ppermute(out_c, "col", beside)
    own = [shaped(TOK, HD), shaped(TOK, PAIR), shaped(TOK, PAIR)]
    mix, top, tot = call(own_kernel, own, "own", [VMEM] * 7, flags, q, kva, kvb, *state)
    (out,) = call(
        merge_kernel, [shaped(TOK, HD, dtype=BF16)], "merge", [VMEM] * 6, flags, mix, top, tot, in_d, in_c
    )
    return out.reshape(1, 1, TOK, HD)


def solution(mesh):
    return jax.shard_map(
        on_device,
        mesh=mesh,
        in_specs=(
            P("row", "col", None, None),
            P("row", "col", None, None),
            P("row", "col", None, None),
            P(),
        ),
        out_specs=P("row", "col", None, None),
        check_vma=False,
    )
```

```python
import functools

import jax
import jax.numpy as jnp
from jax import lax
from jax.experimental import pallas as pl
from jax.experimental.pallas import tpu as pltpu
from jax.sharding import PartitionSpec as P

HDIM = 64
HEADS = 12
PAIR = 2 * HDIM
PAIRS = HEADS // 2
TOK = 128
HD = HEADS * HDIM
LOG2E = 1.4426950408889634
SCALE = HDIM ** (-0.5) * LOG2E
NEG = -1e30
FLOOR = -1e20
VMEM = pl.BlockSpec(memory_space=pltpu.VMEM)
ANY = pl.BlockSpec(memory_space=pl.ANY)
SMEM = pl.BlockSpec(memory_space=pltpu.SMEM)
F32 = jnp.float32
BF16 = jnp.bfloat16


def swaps(count, first):
    pairs = []
    for i in range(first, count - 1, 2):
        pairs += [(i, i + 1), (i + 1, i)]
    return pairs


def partner(i, odd):
    return ((i + 1) ^ 1) - 1 if odd else i ^ 1


def lane_low():
    return lax.broadcasted_iota(jnp.int32, (TOK, PAIR), 1) < HDIM


def position():
    return lax.axis_index("row"), lax.axis_index("col")


def tile_bias(tissue, row, col):
    rows, cols = tissue.shape
    inside = (row >= 0) & (row < rows)
    at = tissue[jnp.clip(row, 0, rows - 1), col]
    return jnp.where(inside & (at > 0), 0.0, NEG).astype(F32)


def attend(query, tiles, biases):
    low = lane_low()
    bias = jnp.concatenate(biases, axis=1)
    scores, weights, tops, results = [], [], [], []
    for p in range(PAIRS):
        part = query[:, lanes(p)]
        zero = jnp.zeros_like(part)
        both = jnp.concatenate([jnp.where(low, part, zero), jnp.where(low, zero, part)], axis=0)
        keys = jnp.concatenate([tile[:TOK, lanes(p)] for tile in tiles], axis=0)
        product = lax.dot_general(both, keys, (((1,), (1,)), ((), ())), preferred_element_type=F32)
        scores.append(product * SCALE + bias)
    for s in scores:
        top = jnp.maximum(jnp.max(s, axis=1, keepdims=True), FLOOR)
        tops.append(top)
        weights.append(jnp.exp2(s - top).astype(BF16))
    for p, (top, w) in enumerate(zip(tops, weights)):
        values = jnp.concatenate([tile[TOK:, lanes(p)] for tile in tiles], axis=0)
        mixed = jnp.dot(
            w, jnp.concatenate([values, jnp.ones_like(values)], axis=1), preferred_element_type=F32
        )
        shape = (TOK, PAIR)
        results.append((
            jnp.where(low, jnp.broadcast_to(top[:TOK], shape), jnp.broadcast_to(top[TOK:], shape)),
            jnp.where(low, mixed[:TOK, PAIR:], mixed[TOK:, PAIR:]),
            jnp.where(low, mixed[:TOK, :PAIR], mixed[TOK:, :PAIR]),
        ))
    return results


def lanes(p):
    return slice(p * PAIR, (p + 1) * PAIR)


def own_tile(query, kv, bias, top_ref, tot_ref, mix_ref):
    for p, (top, total, mixed) in enumerate(attend(query, (kv,), (bias,))):
        top_ref[:, lanes(p)] = top
        tot_ref[:, lanes(p)] = total
        mix_ref[:, lanes(p)] = mixed


def early_kernel(cols, tissue, q, kv, top_ref, tot_ref, mix_ref, flags):
    row, col = position()
    own = tile_bias(tissue, row, col)
    near = tile_bias(tissue, partner(row, False), col)
    far = tile_bias(tissue, partner(row, True), col)
    other = partner(col, True)
    missing = jnp.where((other >= 0) & (other < cols), 0.0, NEG).astype(F32)
    shown = jnp.where(tissue[row, col] > 0, 1.0, 0.0).astype(F32)
    for n, value in enumerate((near, far, missing, shown, own)):
        flags[n : n + 1, :] = jnp.full((1, PAIR), value, F32)
    own_tile(q, kv, jnp.zeros((1, PAIR), F32), top_ref, tot_ref, mix_ref)


def neighbour_kernel(flags, query, kv, *refs):
    own_tile(query, kv, flags[4:5, :], *refs[-3:])


def attend_late(query, kva, kvb, flags, top, tot, mix):
    for p, (t, l, m) in enumerate(attend(query, (kva, kvb), (flags[0:1, :], flags[1:2, :]))):
        t0 = top[:, lanes(p)]
        best = jnp.maximum(t, t0)
        new, old = jnp.exp2(t - best), jnp.exp2(t0 - best)
        yield p, best, l * new + tot[:, lanes(p)] * old, m * new + mix[:, lanes(p)] * old


def spot(p):
    return (lax.broadcasted_iota(jnp.int32, (TOK, PAIR), 1) & (HDIM - 1)) == p


def pieces(x, count):
    parts = []
    for _ in range(count):
        part = x.astype(BF16).astype(F32)
        parts.append(part)
        x = x - part
    return parts


def side_kernel(flags, query, kva, kvb, top, tot, mix, out):
    tops = jnp.zeros((TOK, PAIR), F32)
    tots = jnp.zeros((TOK, PAIR), F32)
    for p, best, total, mixed in attend_late(query, kva, kvb, flags, top, tot, mix):
        out[:TOK, lanes(p)] = mixed.astype(BF16)
        tops = jnp.where(spot(p), best, tops)
        tots = jnp.where(spot(p), total, tots)
    stats = jnp.zeros((TOK, PAIR), F32)
    for slot, piece in enumerate(pieces(tops, 3) + pieces(tots, 2)):
        stats = stats + (pltpu.roll(piece, 8 * slot, 1) if slot else piece)
    out[:TOK, HD:] = stats.astype(BF16)
    if out.shape[0] > TOK:
        out[TOK:, :] = jnp.zeros((out.shape[0] - TOK, HD + PAIR), BF16)


def own_kernel(flags, q, kva, kvb, top, tot, mix, mix_out, top_out, tot_out):
    tops = jnp.zeros((TOK, PAIR), F32)
    tots = jnp.ones((TOK, PAIR), F32)
    for p, best, total, mixed in attend_late(q, kva, kvb, flags, top, tot, mix):
        mix_out[:, lanes(p)] = mixed
        tops = jnp.where(spot(p), best, tops)
        tots = jnp.where(spot(p), total, tots)
    top_out[...] = tops
    tot_out[...] = tots


def merge_kernel(flags, mix, top, tot, in_d, in_c, out):
    missing, own = flags[2:3, :], flags[3:4, :]
    tops, tots = [top[...]], [tot[...]]
    for part, gap in ((in_c, None), (in_d, missing)):
        stats = part[:TOK, HD:].astype(F32)
        slots = [stats] + [pltpu.roll(stats, PAIR - 8 * slot, 1) for slot in range(1, 5)]
        highest = slots[0] + slots[1] + slots[2]
        tops.append(highest if gap is None else highest + gap)
        tots.append(slots[3] + slots[4])
    best = functools.reduce(jnp.maximum, tops)
    shares = [jnp.exp2(t - best) for t in tops]
    total = functools.reduce(jnp.add, [s * t for s, t in zip(shares, tots)])
    keep = (lax.broadcasted_iota(jnp.int32, (TOK, PAIR), 1) & (HDIM - 1)) < PAIRS
    shares = [jnp.where(keep, s * own / total, 0.0) for s in shares]
    source = lax.broadcasted_iota(jnp.int32, (PAIR, HD), 0)
    target = lax.broadcasted_iota(jnp.int32, (PAIR, HD), 1)
    pick = (source == (target // PAIR + (target & HDIM))).astype(BF16)
    pick = jnp.concatenate([pick, pick], axis=0)
    spread = [
        jnp.dot(jnp.concatenate(pieces(s, 2), axis=1).astype(BF16), pick, preferred_element_type=F32) for s in shares
    ]
    for p in range(PAIRS):
        at = lanes(p)
        acc = None
        for factors, part in zip(spread, (mix, in_c, in_d)):
            term = factors[:, at] * part[:TOK, at].astype(F32)
            acc = term if acc is None else acc + term
        out[:, at] = acc.astype(BF16)


def call(body, outs, name, specs, *args, scratch=()):
    return pl.pallas_call(
        body,
        out_shape=outs,
        in_specs=specs,
        out_specs=[VMEM] * len(outs),
        scratch_shapes=scratch,
        name=name,
        compiler_params=pltpu.CompilerParams(vmem_limit_bytes=16 << 20),
        cost_estimate=pl.CostEstimate(flops=1, transcendentals=0, bytes_accessed=1024),
    )(*args)


def shaped(*shape, dtype=F32):
    return jax.ShapeDtypeStruct(shape, dtype)


def on_device(query_states, key_states, value_states, tissue):
    q, k, v = (a.reshape(TOK, HD) for a in (query_states, key_states, value_states))
    rows, cols = tissue.shape
    far, near = swaps(rows, 1), swaps(rows, 0)
    beyond, beside = swaps(cols, 1), swaps(cols, 0)
    stack = jnp.concatenate([k, v])
    kvb = lax.ppermute(stack, "row", far)
    kva = lax.ppermute(stack, "row", near)
    qd = lax.ppermute(q, "col", beyond)
    qc = lax.ppermute(q, "col", beside)
    outs = [shaped(TOK, HD)] * 3
    *state, flags = call(
        functools.partial(early_kernel, cols), outs + [shaped(8, PAIR)], "early", [SMEM, VMEM, VMEM],
        tissue, q, stack,
    )
    state_c = call(neighbour_kernel, outs, "neighbour", [VMEM] * 3, flags, qc, stack)
    state_d = call(neighbour_kernel, outs, "neighbour", [VMEM] * 3 + [ANY], flags, qd, stack, state_c[0])
    pack = shaped(TOK, HD + PAIR, dtype=BF16)
    pack_d = shaped(TOK + 8, HD + PAIR, dtype=BF16)
    (out_d,) = call(side_kernel, [pack_d], "beyond", [VMEM] * 7, flags, qd, kva, kvb, *state_d)
    in_d = lax.ppermute(out_d, "col", beyond)
    (out_c,) = call(side_kernel, [pack], "beside", [VMEM] * 7, flags, qc, kva, kvb, *state_c)
    in_c = lax.ppermute(out_c, "col", beside)
    own = [shaped(TOK, HD), shaped(TOK, PAIR), shaped(TOK, PAIR)]
    mix, top, tot = call(own_kernel, own, "own", [VMEM] * 7, flags, q, kva, kvb, *state)
    (out,) = call(
        merge_kernel, [shaped(TOK, HD, dtype=BF16)], "merge", [VMEM] * 6, flags, mix, top, tot, in_d, in_c
    )
    return out.reshape(1, 1, TOK, HD)


def solution(mesh):
    return jax.shard_map(
        on_device,
        mesh=mesh,
        in_specs=(
            P("row", "col", None, None),
            P("row", "col", None, None),
            P("row", "col", None, None),
            P(),
        ),
        out_specs=P("row", "col", None, None),
        check_vma=False,
    )
```

```python
import functools

import jax
import jax.numpy as jnp
from jax import lax
from jax.experimental import pallas as pl
from jax.experimental.pallas import tpu as pltpu
from jax.sharding import PartitionSpec as P

HDIM = 64
HEADS = 12
PAIR = 2 * HDIM
PAIRS = HEADS // 2
TOK = 128
HD = HEADS * HDIM
LOG2E = 1.4426950408889634
SCALE = HDIM ** (-0.5) * LOG2E
NEG = -1e30
FLOOR = -1e20
VMEM = pl.BlockSpec(memory_space=pltpu.VMEM)
ANY = pl.BlockSpec(memory_space=pl.ANY)
SMEM = pl.BlockSpec(memory_space=pltpu.SMEM)
F32 = jnp.float32
BF16 = jnp.bfloat16


def swaps(count, first):
    pairs = []
    for i in range(first, count - 1, 2):
        pairs += [(i, i + 1), (i + 1, i)]
    return pairs


def partner(i, odd):
    return ((i + 1) ^ 1) - 1 if odd else i ^ 1


def lane_low():
    return lax.broadcasted_iota(jnp.int32, (TOK, PAIR), 1) < HDIM


def position():
    return lax.axis_index("row"), lax.axis_index("col")


def tile_bias(tissue, row, col):
    rows, cols = tissue.shape
    inside = (row >= 0) & (row < rows)
    at = tissue[jnp.clip(row, 0, rows - 1), col]
    return jnp.where(inside & (at > 0), 0.0, NEG).astype(F32)


def attend(query, tiles, biases):
    low = lane_low()
    bias = jnp.concatenate(biases, axis=1)
    scores, weights, tops, results = [], [], [], []
    for p in range(PAIRS):
        part = query[:, lanes(p)]
        zero = jnp.zeros_like(part)
        both = jnp.concatenate([jnp.where(low, part, zero), jnp.where(low, zero, part)], axis=0)
        keys = jnp.concatenate([tile[:TOK, lanes(p)] for tile in tiles], axis=0)
        product = lax.dot_general(both, keys, (((1,), (1,)), ((), ())), preferred_element_type=F32)
        scores.append(product * SCALE + bias)
    for s in scores:
        top = jnp.maximum(jnp.max(s, axis=1, keepdims=True), FLOOR)
        tops.append(top)
        weights.append(jnp.exp2(s - top).astype(BF16))
    for p, (top, w) in enumerate(zip(tops, weights)):
        values = jnp.concatenate([tile[TOK:, lanes(p)] for tile in tiles], axis=0)
        mixed = jnp.dot(
            w, jnp.concatenate([values, jnp.ones_like(values)], axis=1), preferred_element_type=F32
        )
        shape = (TOK, PAIR)
        results.append((
            jnp.where(low, jnp.broadcast_to(top[:TOK], shape), jnp.broadcast_to(top[TOK:], shape)),
            jnp.where(low, mixed[:TOK, PAIR:], mixed[TOK:, PAIR:]),
            jnp.where(low, mixed[:TOK, :PAIR], mixed[TOK:, :PAIR]),
        ))
    return results


def lanes(p):
    return slice(p * PAIR, (p + 1) * PAIR)


def own_tile(query, kv, bias, top_ref, tot_ref, mix_ref):
    for p, (top, total, mixed) in enumerate(attend(query, (kv,), (bias,))):
        top_ref[:, lanes(p)] = top
        tot_ref[:, lanes(p)] = total
        mix_ref[:, lanes(p)] = mixed


def early_kernel(cols, tissue, q, kv, top_ref, tot_ref, mix_ref, flags):
    row, col = position()
    own = tile_bias(tissue, row, col)
    near = tile_bias(tissue, partner(row, False), col)
    far = tile_bias(tissue, partner(row, True), col)
    other = partner(col, True)
    missing = jnp.where((other >= 0) & (other < cols), 0.0, NEG).astype(F32)
    shown = jnp.where(tissue[row, col] > 0, 1.0, 0.0).astype(F32)
    for n, value in enumerate((near, far, missing, shown, own)):
        flags[n : n + 1, :] = jnp.full((1, PAIR), value, F32)
    own_tile(q, kv, jnp.zeros((1, PAIR), F32), top_ref, tot_ref, mix_ref)


def neighbour_kernel(flags, query, kv, *refs):
    own_tile(query, kv, flags[4:5, :], *refs[-3:])


def attend_late(query, kva, kvb, flags, top, tot, mix):
    for p, (t, l, m) in enumerate(attend(query, (kva, kvb), (flags[0:1, :], flags[1:2, :]))):
        t0 = top[:, lanes(p)]
        best = jnp.maximum(t, t0)
        new, old = jnp.exp2(t - best), jnp.exp2(t0 - best)
        yield p, best, l * new + tot[:, lanes(p)] * old, m * new + mix[:, lanes(p)] * old


def spot(p):
    return (lax.broadcasted_iota(jnp.int32, (TOK, PAIR), 1) & (HDIM - 1)) == p


def pieces(x, count):
    parts = []
    for _ in range(count):
        part = x.astype(BF16).astype(F32)
        parts.append(part)
        x = x - part
    return parts


def partial_sums(out, flags, query, kva, kvb, top, tot, mix):
    tops = jnp.zeros((TOK, PAIR), F32)
    tots = jnp.zeros((TOK, PAIR), F32)
    for p, best, total, mixed in attend_late(query, kva, kvb, flags, top, tot, mix):
        out[:TOK, lanes(p)] = mixed.astype(BF16)
        tops = jnp.where(spot(p), best, tops)
        tots = jnp.where(spot(p), total, tots)
    stats = jnp.zeros((TOK, PAIR), F32)
    for slot, piece in enumerate(pieces(tops, 3) + pieces(tots, 2)):
        stats = stats + (pltpu.roll(piece, 8 * slot, 1) if slot else piece)
    out[:TOK, HD:] = stats.astype(BF16)


def waits(rows):
    row, col = position()
    return ((col & 1) == 1) & ((row == rows // 2 - 1) | (row == rows // 2))


def beyond_kernel(rows, flags, kva, kvb, qd, top_d, tot_d, mix_d, qc, top_c, tot_c, mix_c, out_d, out_c):
    out_d[TOK:, :] = jnp.zeros((out_d.shape[0] - TOK, HD + PAIR), BF16)
    partial_sums(out_d, flags, qd, kva, kvb, top_d, tot_d, mix_d)

    @pl.when(waits(rows))
    def _():
        partial_sums(out_c, flags, qc, kva, kvb, top_c, tot_c, mix_c)


def beside_kernel(rows, flags, kva, kvb, qc, top_c, tot_c, mix_c, done, out_c):
    del done

    @pl.when(jnp.logical_not(waits(rows)))
    def _():
        partial_sums(out_c, flags, qc, kva, kvb, top_c, tot_c, mix_c)


def own_kernel(flags, q, kva, kvb, top, tot, mix, mix_out, top_out, tot_out):
    tops = jnp.zeros((TOK, PAIR), F32)
    tots = jnp.ones((TOK, PAIR), F32)
    for p, best, total, mixed in attend_late(q, kva, kvb, flags, top, tot, mix):
        mix_out[:, lanes(p)] = mixed
        tops = jnp.where(spot(p), best, tops)
        tots = jnp.where(spot(p), total, tots)
    top_out[...] = tops
    tot_out[...] = tots


def unpack(part):
    stats = part[:TOK, HD:].astype(F32)
    slots = [stats] + [pltpu.roll(stats, PAIR - 8 * slot, 1) for slot in range(1, 5)]
    return slots[0] + slots[1] + slots[2], slots[3] + slots[4]


def spread(share):
    keep = (lax.broadcasted_iota(jnp.int32, (TOK, PAIR), 1) & (HDIM - 1)) < PAIRS
    source = lax.broadcasted_iota(jnp.int32, (PAIR, HD), 0)
    target = lax.broadcasted_iota(jnp.int32, (PAIR, HD), 1)
    pick = (source == (target // PAIR + (target & HDIM))).astype(BF16)
    parts = jnp.concatenate(pieces(jnp.where(keep, share, 0.0), 2), axis=1).astype(BF16)
    return jnp.dot(parts, jnp.concatenate([pick, pick], axis=0), preferred_element_type=F32)


def join_kernel(mix, top, tot, in_c, mix_out, top_out, tot_out):
    other, total = unpack(in_c)
    best = jnp.maximum(top[...], other)
    mine, theirs = jnp.exp2(top[...] - best), jnp.exp2(other - best)
    top_out[...] = best
    tot_out[...] = tot[...] * mine + total * theirs
    mix_out[...] = mix[...] * spread(mine) + in_c[:TOK, :HD].astype(F32) * spread(theirs)


def merge_kernel(flags, mix, top, tot, in_d, out):
    other, total = unpack(in_d)
    other = other + flags[2:3, :]
    best = jnp.maximum(top[...], other)
    mine, theirs = jnp.exp2(top[...] - best), jnp.exp2(other - best)
    factor = flags[3:4, :] / (tot[...] * mine + total * theirs)
    out[...] = (
        mix[...] * spread(mine * factor) + in_d[:TOK, :HD].astype(F32) * spread(theirs * factor)
    ).astype(BF16)


def call(body, outs, name, specs, *args, scratch=(), aliases={}):
    return pl.pallas_call(
        body,
        out_shape=outs,
        in_specs=specs,
        out_specs=[VMEM] * len(outs),
        scratch_shapes=scratch,
        input_output_aliases=aliases,
        name=name,
        compiler_params=pltpu.CompilerParams(vmem_limit_bytes=16 << 20),
        cost_estimate=pl.CostEstimate(flops=1, transcendentals=0, bytes_accessed=1024),
    )(*args)


def shaped(*shape, dtype=F32):
    return jax.ShapeDtypeStruct(shape, dtype)


def on_device(query_states, key_states, value_states, tissue):
    q, k, v = (a.reshape(TOK, HD) for a in (query_states, key_states, value_states))
    rows, cols = tissue.shape
    far, near = swaps(rows, 1), swaps(rows, 0)
    beyond, beside = swaps(cols, 1), swaps(cols, 0)
    stack = jnp.concatenate([k, v])
    kvb = lax.ppermute(stack, "row", far)
    kva = lax.ppermute(stack, "row", near)
    qd = lax.ppermute(q, "col", beyond)
    qc = lax.ppermute(q, "col", beside)
    outs = [shaped(TOK, HD)] * 3
    *state, flags = call(
        functools.partial(early_kernel, cols), outs + [shaped(8, PAIR)], "early", [SMEM, VMEM, VMEM],
        tissue, q, stack,
    )
    state_c = call(neighbour_kernel, outs, "neighbour", [VMEM] * 3, flags, qc, stack)
    state_d = call(neighbour_kernel, outs, "neighbour", [VMEM] * 3 + [ANY], flags, qd, stack, state_c[0])
    pack = shaped(TOK, HD + PAIR, dtype=BF16)
    pack_d = shaped(TOK + 8, HD + PAIR, dtype=BF16)
    out_d, out_c = call(
        functools.partial(beyond_kernel, rows), [pack_d, pack], "beyond", [VMEM] * 11, flags, kva, kvb, qd, *state_d, qc, *state_c
    )
    in_d = lax.ppermute(out_d, "col", beyond)
    (out_c,) = call(
        functools.partial(beside_kernel, rows), [pack], "beside", [VMEM] * 8, flags, kva, kvb, qc, *state_c, out_c, aliases={7: 0}
    )
    in_c = lax.ppermute(out_c, "col", beside)
    own = [shaped(TOK, HD), shaped(TOK, PAIR), shaped(TOK, PAIR)]
    mix, top, tot = call(own_kernel, own, "own", [VMEM] * 7, flags, q, kva, kvb, *state)
    mix, top, tot = call(join_kernel, own, "join", [VMEM] * 4, mix, top, tot, in_c)
    (out,) = call(merge_kernel, [shaped(TOK, HD, dtype=BF16)], "merge", [VMEM] * 5, flags, mix, top, tot, in_d)
    return out.reshape(1, 1, TOK, HD)


def solution(mesh):
    return jax.shard_map(
        on_device,
        mesh=mesh,
        in_specs=(
            P("row", "col", None, None),
            P("row", "col", None, None),
            P("row", "col", None, None),
            P(),
        ),
        out_specs=P("row", "col", None, None),
        check_vma=False,
    )
```

```python
import functools

import jax
import jax.numpy as jnp
from jax import lax
from jax.experimental import pallas as pl
from jax.experimental.pallas import tpu as pltpu
from jax.sharding import PartitionSpec as P

HDIM = 64
HEADS = 12
PAIR = 2 * HDIM
PAIRS = HEADS // 2
TOK = 128
HD = HEADS * HDIM
LOG2E = 1.4426950408889634
SCALE = HDIM ** (-0.5) * LOG2E
NEG = -1e30
FLOOR = -1e20
VMEM = pl.BlockSpec(memory_space=pltpu.VMEM)
ANY = pl.BlockSpec(memory_space=pl.ANY)
SMEM = pl.BlockSpec(memory_space=pltpu.SMEM)
F32 = jnp.float32
BF16 = jnp.bfloat16


def swaps(count, first):
    pairs = []
    for i in range(first, count - 1, 2):
        pairs += [(i, i + 1), (i + 1, i)]
    return pairs


def partner(i, odd):
    return ((i + 1) ^ 1) - 1 if odd else i ^ 1


def lane_low():
    return lax.broadcasted_iota(jnp.int32, (TOK, PAIR), 1) < HDIM


def position():
    return lax.axis_index("row"), lax.axis_index("col")


def tile_bias(tissue, row, col):
    rows, cols = tissue.shape
    inside = (row >= 0) & (row < rows)
    at = tissue[jnp.clip(row, 0, rows - 1), col]
    return jnp.where(inside & (at > 0), 0.0, NEG).astype(F32)


def attend(query, tiles, biases):
    low = lane_low()
    bias = jnp.concatenate(biases, axis=1)
    scores, weights, tops, results = [], [], [], []
    for p in range(PAIRS):
        part = query[:, lanes(p)]
        zero = jnp.zeros_like(part)
        both = jnp.concatenate([jnp.where(low, part, zero), jnp.where(low, zero, part)], axis=0)
        keys = jnp.concatenate([tile[:TOK, lanes(p)] for tile in tiles], axis=0)
        product = lax.dot_general(both, keys, (((1,), (1,)), ((), ())), preferred_element_type=F32)
        scores.append(product * SCALE + bias)
    for s in scores:
        top = jnp.maximum(jnp.max(s, axis=1, keepdims=True), FLOOR)
        tops.append(top)
        weights.append(jnp.exp2(s - top).astype(BF16))
    for p, (top, w) in enumerate(zip(tops, weights)):
        values = jnp.concatenate([tile[TOK:, lanes(p)] for tile in tiles], axis=0)
        mixed = jnp.dot(
            w, jnp.concatenate([values, jnp.ones_like(values)], axis=1), preferred_element_type=F32
        )
        shape = (TOK, PAIR)
        results.append((
            jnp.where(low, jnp.broadcast_to(top[:TOK], shape), jnp.broadcast_to(top[TOK:], shape)),
            jnp.where(low, mixed[:TOK, PAIR:], mixed[TOK:, PAIR:]),
            jnp.where(low, mixed[:TOK, :PAIR], mixed[TOK:, :PAIR]),
        ))
    return results


def lanes(p):
    return slice(p * PAIR, (p + 1) * PAIR)


def own_tile(query, kv, bias, top_ref, tot_ref, mix_ref):
    for p, (top, total, mixed) in enumerate(attend(query, (kv,), (bias,))):
        top_ref[:, lanes(p)] = top
        tot_ref[:, lanes(p)] = total
        mix_ref[:, lanes(p)] = mixed


def early_kernel(cols, tissue, q, kv, top_ref, tot_ref, mix_ref, flags):
    row, col = position()
    own = tile_bias(tissue, row, col)
    near = tile_bias(tissue, partner(row, False), col)
    far = tile_bias(tissue, partner(row, True), col)
    other = partner(col, True)
    missing = jnp.where((other >= 0) & (other < cols), 0.0, NEG).astype(F32)
    shown = jnp.where(tissue[row, col] > 0, 1.0, 0.0).astype(F32)
    for n, value in enumerate((near, far, missing, shown, own)):
        flags[n : n + 1, :] = jnp.full((1, PAIR), value, F32)
    own_tile(q, kv, jnp.zeros((1, PAIR), F32), top_ref, tot_ref, mix_ref)


def neighbour_kernel(flags, query, kv, *refs):
    own_tile(query, kv, flags[4:5, :], *refs[-3:])


def attend_late(query, kva, kvb, flags, top, tot, mix):
    for p, (t, l, m) in enumerate(attend(query, (kva, kvb), (flags[0:1, :], flags[1:2, :]))):
        t0 = top[:, lanes(p)]
        best = jnp.maximum(t, t0)
        new, old = jnp.exp2(t - best), jnp.exp2(t0 - best)
        yield p, best, l * new + tot[:, lanes(p)] * old, m * new + mix[:, lanes(p)] * old


def spot(p):
    return (lax.broadcasted_iota(jnp.int32, (TOK, PAIR), 1) & (HDIM - 1)) == p


def pieces(x, count):
    parts = []
    for _ in range(count):
        part = x.astype(BF16).astype(F32)
        parts.append(part)
        x = x - part
    return parts


def partial_sums(out, flags, query, kva, kvb, top, tot, mix):
    tops = jnp.zeros((TOK, PAIR), F32)
    tots = jnp.zeros((TOK, PAIR), F32)
    for p, best, total, mixed in attend_late(query, kva, kvb, flags, top, tot, mix):
        out[:TOK, lanes(p)] = mixed.astype(BF16)
        tops = jnp.where(spot(p), best, tops)
        tots = jnp.where(spot(p), total, tots)
    stats = jnp.zeros((TOK, PAIR), F32)
    for slot, piece in enumerate(pieces(tops, 3) + pieces(tots, 2)):
        stats = stats + (pltpu.roll(piece, 8 * slot, 1) if slot else piece)
    out[:TOK, HD:] = stats.astype(BF16)


def waits(rows):
    row, col = position()
    return ((col & 1) == 1) & ((col & 15) != 15) & ((row == rows // 2 - 1) | (row == rows // 2))


def beyond_kernel(rows, flags, kva, kvb, qd, top_d, tot_d, mix_d, qc, top_c, tot_c, mix_c, out_d, out_c):
    out_d[TOK:, :] = jnp.zeros((out_d.shape[0] - TOK, HD + PAIR), BF16)
    partial_sums(out_d, flags, qd, kva, kvb, top_d, tot_d, mix_d)

    @pl.when(waits(rows))
    def _():
        partial_sums(out_c, flags, qc, kva, kvb, top_c, tot_c, mix_c)


def beside_kernel(rows, flags, kva, kvb, qc, top_c, tot_c, mix_c, done, out_c):
    del done

    @pl.when(jnp.logical_not(waits(rows)))
    def _():
        partial_sums(out_c, flags, qc, kva, kvb, top_c, tot_c, mix_c)


def own_kernel(flags, q, kva, kvb, top, tot, mix, mix_out, top_out, tot_out):
    tops = jnp.zeros((TOK, PAIR), F32)
    tots = jnp.ones((TOK, PAIR), F32)
    for p, best, total, mixed in attend_late(q, kva, kvb, flags, top, tot, mix):
        mix_out[:, lanes(p)] = mixed
        tops = jnp.where(spot(p), best, tops)
        tots = jnp.where(spot(p), total, tots)
    top_out[...] = tops
    tot_out[...] = tots


def unpack(part):
    stats = part[:TOK, HD:].astype(F32)
    slots = [stats] + [pltpu.roll(stats, PAIR - 8 * slot, 1) for slot in range(1, 5)]
    return slots[0] + slots[1] + slots[2], slots[3] + slots[4]


def spread(share):
    keep = (lax.broadcasted_iota(jnp.int32, (TOK, PAIR), 1) & (HDIM - 1)) < PAIRS
    source = lax.broadcasted_iota(jnp.int32, (PAIR, HD), 0)
    target = lax.broadcasted_iota(jnp.int32, (PAIR, HD), 1)
    pick = (source == (target // PAIR + (target & HDIM))).astype(BF16)
    parts = jnp.concatenate(pieces(jnp.where(keep, share, 0.0), 2), axis=1).astype(BF16)
    return jnp.dot(parts, jnp.concatenate([pick, pick], axis=0), preferred_element_type=F32)


def join_kernel(mix, top, tot, in_c, mix_out, top_out, tot_out):
    other, total = unpack(in_c)
    best = jnp.maximum(top[...], other)
    mine, theirs = jnp.exp2(top[...] - best), jnp.exp2(other - best)
    top_out[...] = best
    tot_out[...] = tot[...] * mine + total * theirs
    mix_out[...] = mix[...] * spread(mine) + in_c[:TOK, :HD].astype(F32) * spread(theirs)


def merge_kernel(flags, mix, top, tot, in_d, out):
    other, total = unpack(in_d)
    other = other + flags[2:3, :]
    best = jnp.maximum(top[...], other)
    mine, theirs = jnp.exp2(top[...] - best), jnp.exp2(other - best)
    factor = flags[3:4, :] / (tot[...] * mine + total * theirs)
    out[...] = (
        mix[...] * spread(mine * factor) + in_d[:TOK, :HD].astype(F32) * spread(theirs * factor)
    ).astype(BF16)


def call(body, outs, name, specs, *args, scratch=(), aliases={}):
    return pl.pallas_call(
        body,
        out_shape=outs,
        in_specs=specs,
        out_specs=[VMEM] * len(outs),
        scratch_shapes=scratch,
        input_output_aliases=aliases,
        name=name,
        compiler_params=pltpu.CompilerParams(vmem_limit_bytes=16 << 20),
        cost_estimate=pl.CostEstimate(flops=1, transcendentals=0, bytes_accessed=1024),
    )(*args)


def shaped(*shape, dtype=F32):
    return jax.ShapeDtypeStruct(shape, dtype)


def on_device(query_states, key_states, value_states, tissue):
    q, k, v = (a.reshape(TOK, HD) for a in (query_states, key_states, value_states))
    rows, cols = tissue.shape
    far, near = swaps(rows, 1), swaps(rows, 0)
    beyond, beside = swaps(cols, 1), swaps(cols, 0)
    stack = jnp.concatenate([k, v])
    kvb = lax.ppermute(stack, "row", far)
    kva = lax.ppermute(stack, "row", near)
    qd = lax.ppermute(q, "col", beyond)
    qc = lax.ppermute(q, "col", beside)
    outs = [shaped(TOK, HD)] * 3
    *state, flags = call(
        functools.partial(early_kernel, cols), outs + [shaped(8, PAIR)], "early", [SMEM, VMEM, VMEM],
        tissue, q, stack,
    )
    state_c = call(neighbour_kernel, outs, "neighbour", [VMEM] * 3, flags, qc, stack)
    state_d = call(neighbour_kernel, outs, "neighbour", [VMEM] * 3 + [ANY], flags, qd, stack, state_c[0])
    pack = shaped(TOK, HD + PAIR, dtype=BF16)
    pack_d = shaped(TOK + 8, HD + PAIR, dtype=BF16)
    out_d, out_c = call(
        functools.partial(beyond_kernel, rows), [pack_d, pack], "beyond", [VMEM] * 11, flags, kva, kvb, qd, *state_d, qc, *state_c
    )
    in_d = lax.ppermute(out_d, "col", beyond)
    (out_c,) = call(
        functools.partial(beside_kernel, rows), [pack], "beside", [VMEM] * 8, flags, kva, kvb, qc, *state_c, out_c, aliases={7: 0}
    )
    in_c = lax.ppermute(out_c, "col", beside)
    own = [shaped(TOK, HD), shaped(TOK, PAIR), shaped(TOK, PAIR)]
    mix, top, tot = call(own_kernel, own, "own", [VMEM] * 7, flags, q, kva, kvb, *state)
    mix, top, tot = call(join_kernel, own, "join", [VMEM] * 4, mix, top, tot, in_c)
    (out,) = call(merge_kernel, [shaped(TOK, HD, dtype=BF16)], "merge", [VMEM] * 5, flags, mix, top, tot, in_d)
    return out.reshape(1, 1, TOK, HD)


def solution(mesh):
    return jax.shard_map(
        on_device,
        mesh=mesh,
        in_specs=(
            P("row", "col", None, None),
            P("row", "col", None, None),
            P("row", "col", None, None),
            P(),
        ),
        out_specs=P("row", "col", None, None),
        check_vma=False,
    )
```
